128 devices in a mesh: elec: 8 (over y_lo, z), cell: 16 (over y_hi, x, core).
Axes of the slice: x: 4, y: 4 (y_hi: 2, y_lo: 2; y = y_hi * 2 + y_lo), z: 4, core: 2. Of those that a mesh axis runs over, the one named last changes fastest.
Arguments:
- grads: bfloat16 [3, 1024, 2048], P(None, 'elec', 'cell'), may hold values from -6 to 6
- quads: int32 [32768, 4], P('elec'), may hold values from 0 to 1023, all different within a row
- volume: float32 [2048], P('cell'), may hold values from 0.5 to 2
- weight: float32 [32768], P('elec'), may hold values from 0.5 to 2
Outputs:
- hessian: float32 [2048, 2048], P('elec', 'cell')
The draws below stay inside these ranges and needn't reach their ends.
Inputs may be any that keep to these rules, and one draw needn't show every extreme that they name: `quads`: each row names four different electrodes; every electrode appears in some row.
All inputs are finite; a program needn't handle non-finite values.
Results may differ from the reference program's by a relative error of at most 0.00096.
Values may be sent and summed in bfloat16 or wider, within the bound.
A program may use at most 64 MiB of HBM per device.

```python
import math
import jax
import jax.numpy as jnp
from jax import lax

ELECTRODE_COUNT = 1024
SLAB_CELLS = 2048
MEASURE_TOTAL = 32768


def steps_of(own_key, dims, shards, low, largest):
    factor_of, own = 1.0, jax.random.fold_in(own_key, 6)
    for axis_at, blocks in shards:
        steps = jnp.exp(jax.random.uniform(jax.random.fold_in(own, axis_at), (blocks,), jnp.float32, low / len(shards), largest / len(shards)))
        factor_of = factor_of * jnp.repeat(steps, dims[axis_at] // blocks).reshape([-1 if axis == axis_at else 1 for axis in range(len(dims))])
    return factor_of


def distinct(own_key, rows, amount, top, lift):
    order = jax.random.permutation(jax.random.fold_in(own_key, 1), amount)
    pull = order
    for power in range(3):
        pull = pull * pull // amount
    pull = pull * lift // amount
    lots = jax.random.randint(jax.random.fold_in(own_key, 2), (rows, amount), 0, 4096) + pull
    sure = jax.random.permutation(jax.random.fold_in(own_key, 3), rows)[jnp.arange(amount) % rows]
    lots = jnp.where(jnp.arange(rows)[:, None] == sure[None, :], 1 << 14, lots)
    merit = lots * amount + jnp.arange(amount)
    return lax.top_k(merit.astype(jnp.int32), top)[1].astype(jnp.int32)


def gaussian(stream_key, extent, deviation, most, split=(), dtype=jnp.bfloat16):
    array = deviation * jax.random.normal(stream_key, extent, jnp.float32)
    if split:
        array = array * steps_of(stream_key, extent, split, -0.22, 0.18)
    return jnp.clip(array, -most, most).astype(dtype)


def setup_inputs(seed: int = 0) -> dict:
    streams_of = jax.random.split(jax.random.key(seed), 5)
    grads = gaussian(streams_of[0], (3, ELECTRODE_COUNT, SLAB_CELLS), 1.0, 6.0, ((1, 8), (2, 16)))
    quads = distinct(streams_of[1], MEASURE_TOTAL, ELECTRODE_COUNT, 4, 0)
    volume = jnp.clip(jnp.exp(math.log(2.0) - 1.3862944 * jax.random.uniform(streams_of[2], (SLAB_CELLS,), jnp.float32) ** steps_of(streams_of[2], (SLAB_CELLS,), ((0, 16),), -0.2, 0.2)), 0.5, 2.0)
    weight = jnp.clip(jnp.exp(math.log(2.0) - 1.3862944 * jax.random.uniform(streams_of[3], (MEASURE_TOTAL,), jnp.float32) ** steps_of(streams_of[3], (MEASURE_TOTAL,), ((0, 8),), -0.2, 0.2)), 0.5, 2.0)
    return dict(grads=grads, quads=quads, volume=volume, weight=weight)


def reference(grads, quads, volume, weight):
    field = grads.astype(jnp.float32)
    rows_of_block = math.gcd(MEASURE_TOTAL, 1024)

    def single_block(index):
        begin = (index * rows_of_block).astype(jnp.int32)
        rows = lax.dynamic_slice_in_dim(quads, begin, rows_of_block, 0)
        gains = lax.dynamic_slice_in_dim(weight, begin, rows_of_block, 0)
        source = field[:, rows[:, 0], :] - field[:, rows[:, 1], :]
        receiver = field[:, rows[:, 2], :] - field[:, rows[:, 3], :]
        dots = source[0] * receiver[0] + source[1] * receiver[1] + source[2] * receiver[2]
        return (gains[:, None] * (-(volume[None, :] * dots))).astype(jnp.bfloat16)

    scaled_rows = lax.map(single_block, jnp.arange(MEASURE_TOTAL // rows_of_block).astype(jnp.int32))
    scaled_rows = scaled_rows.reshape(MEASURE_TOTAL, SLAB_CELLS).astype(jnp.float32)
    total_hessian = jnp.dot(scaled_rows.T, scaled_rows, precision=lax.Precision.HIGHEST, preferred_element_type=jnp.float32)
    return total_hessian / jnp.float32(MEASURE_TOTAL)
```

```python
import functools

import jax
import jax.numpy as jnp
from jax import lax
from jax.experimental import pallas as pl
from jax.experimental.pallas import tpu as pltpu
from jax.sharding import PartitionSpec as P

MESH = pl.DeviceIdType.MESH
NT = (((1,), (1,)), ((), ()))
EARLY = [(0, 0), (0, 1), (1, 0), (2, 0), (3, 0)]
LATE = [(1, 1), (2, 1), (3, 1), (4, 0), (4, 1), (5, 0), (5, 1)]
BLOCKS = EARLY + LATE
STEPS = [(0, 1), (0, 3), (1, 0), (0, 2), (1, 1), (1, 3), (1, 2)]
ROWS = [(0, 0), (0, 1), (0, 2), (1, 0), (1, 0), (1, 0)]
COLS = [(0, 0), (0, 0), (0, 0), (0, 0), (0, 1), (0, 2)]


def dot_nt(left, right):
    return lax.dot_general(left, right, NT, preferred_element_type=jnp.float32)


def kernel(
    g_ref, q_ref, v_ref, w_ref, out_ref,
    gt, vol, vb, ms, mr, a, b, cc, y, v, sums, part, own, strips, fin, dd, tt,
    ready, gs, gr, ps, pr, bs, br, ys, yr, vs, vr, cs, cr, ks, kr, rs, rr, fs, ts, fr, tr,
):
    e = lax.axis_index("elec")
    cell = lax.axis_index("cell")
    ylo, z = e // 4, e % 4
    yhi, x, c = cell // 8, (cell // 2) % 4, cell % 2
    half_x = x // 2
    half_y = yhi

    def at(dy, dx, core):
        return (((yhi + dy) % 2) * 4 + (x + dx) % 4) * 2 + core

    def group(dy, dx):
        return ((yhi + dy) % 2) * 4 + (x + dx) % 4

    def send(src, dst, ssem, rsem, to):
        return pltpu.make_async_remote_copy(
            src, dst, ssem, rsem, device_id=to, device_id_type=MESH
        )

    barrier = pltpu.get_barrier_semaphore()
    for step in range(1, 8):
        pl.semaphore_signal(barrier, inc=1, device_id=((e + step) % 8, cell), device_id_type=MESH)
    for step in range(1, 16):
        pl.semaphore_signal(barrier, inc=1, device_id=(e, (cell + step) % 16), device_id_type=MESH)

    own_columns = pl.ds(pl.multiple_of(e * 128, 128), 128)
    for k in range(3):
        gt[c, pl.ds(k * 128, 128), own_columns] = g_ref[k].T
    vol[c] = jnp.broadcast_to(v_ref[...], (8, 128))
    pl.semaphore_wait(barrier, 22)
    for step in range(1, 16):
        pl.semaphore_signal(ready, inc=1, device_id=(e, (cell + step) % 16), device_id_type=MESH)

    def peer(i):
        dy, dz = STEPS[i]
        return ((ylo + dy) % 2) * 4 + (z + dz) % 4

    def source(i):
        dy, dz = STEPS[i]
        return ((ylo + dy) % 2) * 4 + (z + 4 - dz) % 4

    def piece(electrode_group):
        return gt.at[c, :, pl.ds(pl.multiple_of(electrode_group * 128, 128), 128)]

    partner = (e, at(0, 0, 1 - c))
    gathers = [
        send(piece(e), piece(e), gs.at[i], gr.at[i], (peer(i), cell)) for i in range(7)
    ]
    for copy in gathers:
        copy.start()
    volume_copy = send(vol.at[c], vol.at[c], ps.at[8], pr.at[8], partner)
    volume_copy.start()
    passes = [send(piece(e), piece(e), ps.at[7], pr.at[7], partner)]
    passes[0].start()

    base = pl.multiple_of(c * 2048, 2048)
    electrodes = [q_ref[pl.ds(k, 1), pl.ds(base, 2048)] for k in range(4)]

    def maps(row, carry):
        first = pl.multiple_of(row * 16, 16)
        label = lax.broadcasted_iota(jnp.int32, (16, 2048), 0) + first
        one = jnp.float32(1)
        ms[pl.ds(first, 16), :] = jnp.where(
            label == electrodes[0], one, jnp.where(label == electrodes[1], -one, 0.0)
        ).astype(jnp.bfloat16)
        mr[pl.ds(first, 16), :] = jnp.where(
            label == electrodes[2], one, jnp.where(label == electrodes[3], -one, 0.0)
        ).astype(jnp.bfloat16)
        return carry

    lax.fori_loop(0, 64, maps, 0)
    for i in range(7):
        gathers[i].wait_recv()
        passes.append(send(piece(source(i)), piece(source(i)), ps.at[i], pr.at[i], partner))
        passes[-1].start()
    volume_copy.wait()
    for h in range(2):
        vb[h] = jnp.broadcast_to(vol[h, 0:1, :], (128, 128)).T
    for copy in passes:
        copy.wait_recv()

    to_b = (e, at(0, 3, c))
    to_v = (e, at(0, 1, c))
    to_y = (e, at(1, 0, c))

    def columns(q, width=512):
        return pl.ds(pl.multiple_of(q * width, width), width)

    def b_copy(h, t, q):
        return send(a.at[h, :, columns(q)], b.at[h, :, columns(q)], bs.at[h * 4 + t], br.at[h * 4 + t], to_b)

    def y_copy(h, t, q):
        return send(a.at[h, :, columns(q)], y.at[h, :, columns(q)], ys.at[h * 4 + t], yr.at[h * 4 + t], to_y)

    def v_copy(h, t, q):
        return send(a.at[h, :, columns(q)], v.at[h, :, columns(t)], vs.at[h * 2 + t], vr.at[h * 2 + t], to_v)

    def c_copy(h, t):
        return send(v.at[h, :, columns(t)], cc.at[h, :, columns(t)], cs.at[h * 2 + t], cr.at[h * 2 + t], to_v)

    def chunk(t):
        return (t + 2 * (1 - half_x)) % 4

    def sensitivities(h, t):
        q = chunk(t)
        cols = columns(q)
        source = jnp.dot(gt[h], ms[:, cols], preferred_element_type=jnp.float32)
        receiver = jnp.dot(gt[h], mr[:, cols], preferred_element_type=jnp.float32)
        dots = (
            source[0:128] * receiver[0:128]
            + source[128:256] * receiver[128:256]
            + source[256:384] * receiver[256:384]
        )
        gain = w_ref[:, pl.ds(pl.multiple_of(base + q * 512, 512), 512)]
        volumes = jnp.concatenate([vb[h]] * 4, axis=1)
        a[h, :, cols] = (gain * -(volumes * dots)).astype(jnp.bfloat16)
        if t < 2:
            v_copy(h, t, q).start()
        b_copy(h, t, q).start()
        y_copy(h, t, q).start()

    for t in range(4):
        sensitivities(0, t)
    for t in range(4):
        sensitivities(1, t)
        if t % 2:
            v_copy(0, t // 2, chunk(t // 2)).wait_recv()
            c_copy(0, t // 2).start()

    def put(block, value):
        sums[0, block] = value[:, 0:128]
        sums[1, block] = value[:, 128:256]

    def a_part(half=None):
        if half is None:
            return a[...].reshape(256, 2048)
        return a[:, :, columns(half, 1024)].reshape(256, 1024)

    whole = dot_nt(a_part(), a_part())
    put(0, whole[0:128])
    put(1, whole[128:256])
    for t in range(2):
        v_copy(1, t, chunk(t)).wait_recv()
        c_copy(1, t).start()

    def arrive(h):
        for t in range(4):
            b_copy(h, t, chunk(t)).wait_recv()
            y_copy(h, t, chunk(t)).wait_recv()
        for t in range(2):
            c_copy(h, t).wait_recv()

    def border(h, first):
        put(first, dot_nt(b[h], a_part()))
        put(first + 1, dot_nt(cc[h], a_part(half_x)))
        put(first + 2, dot_nt(y[h, :, columns(half_y, 1024)], a_part(half_y)))

    def core_copy(late):
        blocks = pl.ds(5, 7) if late else pl.ds(0, 5)
        return send(sums.at[1 - c, blocks], part.at[blocks], ks.at[late], kr.at[late], partner)

    def strip_copy(late, i):
        blocks = pl.ds(5, 7) if late else pl.ds(0, 5)
        rows = pl.ds(pl.multiple_of(peer(i) * 16, 16), 16)
        return send(
            own.at[blocks, rows], strips.at[e, blocks],
            rs.at[late * 8 + i], rr.at[late * 8 + i], (peer(i), cell),
        )

    def strip_arrival(late, i):
        blocks = pl.ds(5, 7) if late else pl.ds(0, 5)
        return send(
            own.at[blocks, pl.ds(0, 16)], strips.at[source(i), blocks],
            rs.at[late * 8 + i], rr.at[late * 8 + i], (source(i), cell),
        )

    def add_cores(late):
        core_copy(late).wait()
        for i in range(12):
            if (i >= 5) == bool(late):
                own[i] = sums[c, i] + part[i]

    def scatter(late):
        for i in range(7):
            strip_copy(late, i).start()

    def gather_strips(late):
        first, last = (5, 12) if late else (0, 5)
        rows = pl.ds(pl.multiple_of(e * 16, 16), 16)
        strips[e, first:last] = own[first:last, rows]
        for i in range(7):
            strip_arrival(late, i).wait_recv()
        total = strips[0, first:last]
        for group_of in range(1, 8):
            total = total + strips[group_of, first:last]
        fin[first:last] = total * jnp.float32(1.0 / 32768)

    def deliver(i, start):
        k, r = BLOCKS[i]
        row_half = r
        offset = pl.multiple_of(e * 16, 16)
        landing = dd.at[pl.ds(pl.multiple_of(row_half * 128 + e * 16, 16), 16)]
        row_group, col_group = group(*ROWS[k]), group(*COLS[k])
        copy = send(fin.at[i], landing, fs.at[i], fr, (row_group, col_group * 2 + c))
        if COLS[k] == (0, 0):
            @pl.when(row_group == e)
            def _():
                if start:
                    pltpu.make_async_copy(fin.at[i], landing, fr).start()

            @pl.when(row_group != e)
            def _():
                if start:
                    copy.start()
                else:
                    copy.wait_send()
        elif start:
            copy.start()
        else:
            copy.wait_send()
        if k:
            mirror = send(
                fin.at[i], tt.at[c, pl.ds(offset, 16)], ts.at[i], tr,
                (col_group, row_group * 2 + row_half),
            )
            if start:
                mirror.start()
            else:
                mirror.wait_send()

    arrive(0)
    border(0, 2)
    core_copy(0).start()
    add_cores(0)
    scatter(0)
    gather_strips(0)
    pl.semaphore_wait(ready, 15)
    for i in range(5):
        deliver(i, True)

    arrive(1)
    border(1, 5)
    whole = dot_nt(y[...].reshape(256, 2048), b[...].reshape(256, 2048))
    put(8, whole[0:128])
    put(9, whole[128:256])
    whole = dot_nt(y[:, :, columns(half_x, 1024)].reshape(256, 1024), cc[...].reshape(256, 1024))
    put(10, whole[0:128])
    put(11, whole[128:256])
    core_copy(1).start()
    add_cores(1)
    scatter(1)
    gather_strips(1)
    for i in range(5, 12):
        deliver(i, True)

    for h in range(2):
        for t in range(4):
            b_copy(h, t, chunk(t)).wait_send()
            y_copy(h, t, chunk(t)).wait_send()
        for t in range(2):
            v_copy(h, t, chunk(t)).wait_send()
            c_copy(h, t).wait_send()
    for late in range(2):
        for i in range(7):
            strip_copy(late, i).wait_send()
    for copy in gathers + passes:
        copy.wait_send()


    row_y, row_x = e // 4, e % 4
    dy, dx = (row_y + 2 - yhi) % 2, (row_x + 4 - x) % 4
    kind = dy * 4 + dx
    mirror_only = (kind == 3) | (kind == 5)
    straight_only = (kind == 0) | (kind == 1) | (kind == 7)

    def wait_straight():
        pltpu.make_async_copy(dd, dd, fr).wait()

    def wait_mirror():
        pltpu.make_async_copy(tt, tt, tr).wait()

    @pl.when(mirror_only)
    def _():
        wait_mirror()
        for h in range(2):
            out_ref[pl.ds(h * 128, 128)] = tt[h].T

    @pl.when(straight_only)
    def _():
        wait_straight()
        out_ref[...] = dd[...]

    @pl.when((kind == 2) | (kind == 4) | (kind == 6))
    def _():
        wait_straight()
        wait_mirror()
        for h in range(2):
            out_ref[pl.ds(h * 128, 128)] = dd[pl.ds(h * 128, 128)] + tt[h].T

    for i in range(12):
        deliver(i, False)


def per_device(grads, quads, volume, weight):
    f32, bf16 = jnp.float32, jnp.bfloat16
    dma = pltpu.SemaphoreType.DMA
    vmem = pl.BlockSpec(memory_space=pltpu.VMEM)
    return pl.pallas_call(
        kernel,
        out_shape=jax.ShapeDtypeStruct((256, 128), f32),
        in_specs=[vmem] * 4,
        out_specs=vmem,
        scratch_shapes=[
            pltpu.VMEM((2, 384, 1024), bf16),
            pltpu.VMEM((2, 8, 128), f32),
            pltpu.VMEM((2, 128, 128), f32),
            pltpu.VMEM((1024, 2048), bf16),
            pltpu.VMEM((1024, 2048), bf16),
            pltpu.VMEM((2, 128, 2048), bf16),
            pltpu.VMEM((2, 128, 2048), bf16),
            pltpu.VMEM((2, 128, 1024), bf16),
            pltpu.VMEM((2, 128, 2048), bf16),
            pltpu.VMEM((2, 128, 1024), bf16),
            pltpu.VMEM((2, 12, 128, 128), f32),
            pltpu.VMEM((12, 128, 128), f32),
            pltpu.VMEM((12, 128, 128), f32),
            pltpu.VMEM((8, 12, 16, 128), f32),
            pltpu.VMEM((12, 16, 128), f32),
            pltpu.VMEM((256, 128), f32),
            pltpu.VMEM((2, 128, 128), f32),
            pltpu.SemaphoreType.REGULAR,
            dma((8,)), dma((8,)), dma((9,)), dma((9,)),
            dma((8,)), dma((8,)), dma((8,)), dma((8,)),
            dma((4,)), dma((4,)), dma((4,)), dma((4,)),
            dma((2,)), dma((2,)), dma((16,)), dma((16,)),
            dma((12,)), dma((12,)), dma, dma,
        ],
        compiler_params=pltpu.CompilerParams(
            collective_id=0, has_side_effects=True, vmem_limit_bytes=60000000
        ),
        name="hessian",
    )(grads, quads.T, volume.reshape(1, 128), weight.reshape(1, 4096))


def solution(mesh):
    placed = (P(None, "elec", "cell"), P("elec", None), P("cell"), P("elec"))
    return jax.shard_map(
        per_device, mesh=mesh, in_specs=placed, out_specs=P("elec", "cell"), check_vma=False
    )
```

```python
import functools

import jax
import jax.numpy as jnp
from jax import lax
from jax.experimental import pallas as pl
from jax.experimental.pallas import tpu as pltpu
from jax.sharding import PartitionSpec as P

MESH = pl.DeviceIdType.MESH
NT = (((1,), (1,)), ((), ()))
EARLY = [(0, 0), (0, 1), (1, 0), (2, 0), (3, 0)]
LATE = [(1, 1), (2, 1), (3, 1), (4, 0), (4, 1), (5, 0), (5, 1)]
BLOCKS = EARLY + LATE
GROUPS = [(0, 5), (5, 5), (10, 2)]
LATER = GROUPS[1:]
STEPS = [(1, 0), (0, 1), (0, 3), (0, 2), (1, 1), (1, 3), (1, 2)]
ROWS = [(0, 0), (0, 1), (0, 2), (1, 0), (1, 0), (1, 0)]
COLS = [(0, 0), (0, 0), (0, 0), (0, 0), (0, 1), (0, 2)]


def dot_nt(left, right):
    return lax.dot_general(left, right, NT, preferred_element_type=jnp.float32)


def kernel(
    g_ref, q_ref, v_ref, w_ref, out_ref,
    gt, vol, vb, ms, mr, a, b, cc, y, v, sums, part, own, strips, fin, dd, tt,
    zparts, zsum, zback, zs, zr, gs, gr, ps, pr, bs, br, ys, yr, vs, vr, cs, cr, ks, kr, rs, rr, fs, ts, fr, tr,
):
    e = lax.axis_index("elec")
    cell = lax.axis_index("cell")
    ylo, z = e // 4, e % 4
    yhi, x, c = cell // 8, (cell // 2) % 4, cell % 2
    half_x = x // 2
    half_y = yhi

    def at(dy, dx, core):
        return (((yhi + dy) % 2) * 4 + (x + dx) % 4) * 2 + core

    def group(dy, dx):
        return ((yhi + dy) % 2) * 4 + (x + dx) % 4

    def send(src, dst, ssem, rsem, to):
        return pltpu.make_async_remote_copy(
            src, dst, ssem, rsem, device_id=to, device_id_type=MESH
        )

    def peer(i):
        dy, dz = STEPS[i]
        return ((ylo + dy) % 2) * 4 + (z + dz) % 4

    def source(i):
        dy, dz = STEPS[i]
        return ((ylo + dy) % 2) * 4 + (z + 4 - dz) % 4

    def piece(group_of):
        return gt.at[c, group_of]

    barrier = pltpu.get_barrier_semaphore()
    partner = (e, at(0, 0, 1 - c))
    near = [(peer(i), cell) for i in range(4)]
    near += [partner, (e, at(0, 1, c)), (e, at(0, 3, c)), (e, at(1, 0, c))]
    for device in near:
        pl.semaphore_signal(barrier, inc=1, device_id=device, device_id_type=MESH)

    for k in range(3):
        gt[c, e, pl.ds(k * 128, 128), :] = g_ref[k].T
    vol[c] = jnp.broadcast_to(v_ref[...], (8, 128))
    pl.semaphore_wait(barrier, len(near))

    def gather_copy(i):
        if i < 4:
            return send(piece(e), piece(e), gs.at[i], gr.at[i], (peer(i), cell))
        there = ylo * 4 + peer(i) % 4
        return send(piece(peer(0)), piece(peer(0)), gs.at[i], gr.at[i], (there, cell))

    def pass_copy(i, core):
        group_of = e if i == 7 else source(i)
        part_of = gt.at[core, group_of]
        return send(part_of, part_of, ps.at[i], pr.at[i], partner)

    def start_gather():
        for i in range(4):
            gather_copy(i).start()
        pass_copy(7, c).start()

    def relay_gather():
        gather_copy(0).wait_recv()
        for i in range(4, 7):
            gather_copy(i).start()

    def pass_on():
        for i in range(7):
            if i:
                gather_copy(i).wait_recv()
            pass_copy(i, c).start()

    def wait_passed():
        for i in range(8):
            pass_copy(i, 1 - c).wait_recv()

    pl.when(c == 0)(start_gather)
    volume_copy = send(vol.at[c], vol.at[c], ps.at[8], pr.at[8], partner)
    volume_copy.start()

    base = pl.multiple_of(c * 2048, 2048)
    electrodes = [q_ref[pl.ds(k, 1), pl.ds(base, 2048)] for k in range(4)]

    def maps(row, carry):
        first = pl.multiple_of(row * 16, 16)
        label = lax.broadcasted_iota(jnp.int32, (16, 2048), 0) + first
        one = jnp.float32(1)
        ms[pl.ds(first, 16), :] = jnp.where(
            label == electrodes[0], one, jnp.where(label == electrodes[1], -one, 0.0)
        ).astype(jnp.bfloat16)
        mr[pl.ds(first, 16), :] = jnp.where(
            label == electrodes[2], one, jnp.where(label == electrodes[3], -one, 0.0)
        ).astype(jnp.bfloat16)
        return carry

    lax.fori_loop(0, 32, maps, 0)
    pl.when(c == 0)(relay_gather)
    lax.fori_loop(32, 64, maps, 0)
    pl.when(c == 1)(start_gather)
    volume_copy.wait()
    for h in range(2):
        vb[h] = jnp.broadcast_to(vol[h, 0:1, :], (128, 128)).T
    pl.when(c == 0)(pass_on)
    pl.when(c == 1)(relay_gather)
    pl.when(c == 1)(wait_passed)

    to_b = (e, at(0, 3, c))
    to_v = (e, at(0, 1, c))
    to_y = (e, at(1, 0, c))

    def columns(q, width=512):
        return pl.ds(pl.multiple_of(q * width, width), width)

    def b_copy(h, q):
        return send(a.at[h, :, columns(q)], b.at[h, :, columns(q)], bs.at[h * 4 + q], br.at[h * 4 + q], to_b)

    def y_copy(h, q):
        return send(a.at[h, :, columns(q)], y.at[h, :, columns(q)], ys.at[h * 4 + q], yr.at[h * 4 + q], to_y)

    def v_copy(h, t, q):
        return send(a.at[h, :, columns(q)], v.at[h, :, columns(t)], vs.at[h * 2 + t], vr.at[h * 2 + t], to_v)

    def c_copy(h, t):
        return send(v.at[h, :, columns(t)], cc.at[h, :, columns(t)], cs.at[h * 2 + t], cr.at[h * 2 + t], to_v)

    def chunk(t):
        return (t + 2 * (1 - half_x)) % 4

    def sensitivities(h, t):
        q = chunk(t)
        cols = columns(q)
        field = jnp.concatenate([gt[h, i] for i in range(8)], axis=1)
        source = jnp.dot(field, ms[:, cols], preferred_element_type=jnp.float32)
        receiver = jnp.dot(field, mr[:, cols], preferred_element_type=jnp.float32)
        dots = (
            source[0:128] * receiver[0:128]
            + source[128:256] * receiver[128:256]
            + source[256:384] * receiver[256:384]
        )
        gain = w_ref[:, pl.ds(pl.multiple_of(base + q * 512, 512), 512)]
        volumes = jnp.concatenate([vb[h]] * 4, axis=1)
        a[h, :, cols] = (gain * -(volumes * dots)).astype(jnp.bfloat16)
        if t < 2 and h == 0:
            v_copy(h, t, q).start()
        if h == 0:
            b_copy(h, q).start()
            y_copy(h, q).start()

    for t in range(4):
        sensitivities(0, t)
    pl.when(c == 1)(pass_on)
    pl.when(c == 0)(wait_passed)
    for t in range(4):
        sensitivities(1, t)
        if t % 2:
            v_copy(0, t // 2, chunk(t // 2)).wait_recv()
            c_copy(0, t // 2).start()

    def put(block, value):
        sums[0, block] = value[:, 0:128]
        sums[1, block] = value[:, 128:256]

    def a_part(half=None):
        if half is None:
            return a[...].reshape(256, 2048)
        return a[:, :, columns(half, 1024)].reshape(256, 1024)

    for t in range(2):
        v_copy(1, t, chunk(t)).start()
    for q in range(4):
        b_copy(1, q).start()
        y_copy(1, q).start()
    whole = dot_nt(a_part(), a_part())
    put(0, whole[0:128])
    put(1, whole[128:256])

    def arrive(h):
        for q in range(4):
            b_copy(h, q).wait_recv()
            y_copy(h, q).wait_recv()
        for t in range(2):
            c_copy(h, t).wait_recv()

    def border(h, first):
        put(first, dot_nt(b[h], a_part()))
        put(first + 1, dot_nt(cc[h], a_part(half_x)))
        put(first + 2, dot_nt(y[h, :, columns(half_y, 1024)], a_part(half_y)))

    def core_copy(group_of):
        first, count = GROUPS[group_of]
        blocks = pl.ds(first, count)
        return send(
            sums.at[1 - c, blocks], part.at[blocks], ks.at[group_of], kr.at[group_of], partner
        )

    def add_cores(group_of):
        core_copy(group_of).wait()
        first, count = GROUPS[group_of]
        for i in range(first, first + count):
            own[i] = (sums[c, i] + part[i]).reshape(2, 4, 16, 128)

    def z_copy(i, receive=False):
        dz = (1, 3, 2)[i]
        there = (z + 4 - dz) % 4 if receive else (z + dz) % 4
        row = there if receive else z
        return send(
            own.at[pl.ds(0, 5), :, there], zparts.at[row], zs.at[i], zr.at[i],
            (ylo * 4 + there, cell),
        )

    def y_fold():
        return send(zsum.at[:, 1 - ylo], zback, zs.at[3], zr.at[3], ((1 - ylo) * 4 + z, cell))

    def fold_early():
        for i in range(3):
            z_copy(i, True).wait_recv()
        total = own[0:5, :, z]
        for i in range(3):
            total = total + zparts[(z + 4 - (1, 3, 2)[i]) % 4]
        zsum[...] = total
        y_fold().start()

    def finish_early():
        y_fold().wait()
        fin[0:5] = (zsum[:, ylo] + zback[...]) * jnp.float32(1.0 / 32768)

    def strip_copy(late, i, receive=False):
        first, count = LATER[late]
        blocks = pl.ds(first, count)
        if receive:
            there, slot = source(i), source(i)
        else:
            there, slot = peer(i), e
        return send(
            own.at[blocks, there // 4, there % 4], strips.at[slot, blocks],
            rs.at[late * 8 + i], rr.at[late * 8 + i], (there, cell),
        )

    def scatter(late):
        for i in range(7):
            strip_copy(late, i).start()

    def gather_strips(late):
        first, count = LATER[late]
        last = first + count
        total = own[first:last, ylo, z]
        for i in range(7):
            strip_copy(late, i, True).wait_recv()
        for i in range(7):
            total = total + strips[source(i), first:last]
        fin[first:last] = total * jnp.float32(1.0 / 32768)

    def deliver(i, start):
        k, r = BLOCKS[i]
        row_half = r
        offset = pl.multiple_of(e * 16, 16)
        landing = dd.at[pl.ds(pl.multiple_of(row_half * 128 + e * 16, 16), 16)]
        row_group, col_group = group(*ROWS[k]), group(*COLS[k])
        copy = send(fin.at[i], landing, fs.at[i], fr, (row_group, col_group * 2 + c))
        if COLS[k] == (0, 0):
            @pl.when(row_group == e)
            def _():
                if start:
                    pltpu.make_async_copy(fin.at[i], landing, fr).start()

            @pl.when(row_group != e)
            def _():
                if start:
                    copy.start()
                else:
                    copy.wait_send()
        elif start:
            copy.start()
        else:
            copy.wait_send()
        if k:
            mirror = send(
                fin.at[i], tt.at[c, pl.ds(offset, 16)], ts.at[i], tr,
                (col_group, row_group * 2 + row_half),
            )
            if start:
                mirror.start()
            else:
                mirror.wait_send()

    arrive(0)
    border(0, 2)
    core_copy(0).start()
    for t in range(2):
        v_copy(1, t, chunk(t)).wait_recv()
        c_copy(1, t).start()
    add_cores(0)
    for i in range(3):
        z_copy(i).start()
    fold_early()

    def halves(ref, half):
        return ref[:, :, columns(half, 1024)].reshape(256, 1024)

    for q in range(2):
        b_copy(1, q).wait_recv()
        y_copy(1, q).wait_recv()
    border_b = dot_nt(b[1, :, 0:1024], a_part(0))
    corner_b = dot_nt(halves(y, 0), halves(b, 0))
    for q in range(2, 4):
        b_copy(1, q).wait_recv()
        y_copy(1, q).wait_recv()
    put(5, border_b + dot_nt(b[1, :, 1024:2048], a_part(1)))
    put(7, dot_nt(y[1, :, columns(half_y, 1024)], a_part(half_y)))
    whole = corner_b + dot_nt(halves(y, 1), halves(b, 1))
    put(8, whole[0:128])
    put(9, whole[128:256])
    for t in range(2):
        c_copy(1, t).wait_recv()
    put(6, dot_nt(cc[1], a_part(half_x)))
    core_copy(1).start()
    whole = dot_nt(halves(y, half_x), cc[...].reshape(256, 1024))
    put(10, whole[0:128])
    put(11, whole[128:256])
    core_copy(2).start()
    add_cores(1)
    scatter(0)
    add_cores(2)
    scatter(1)
    finish_early()
    for i in range(5):
        deliver(i, True)
    gather_strips(0)
    for i in range(5, 10):
        deliver(i, True)
    gather_strips(1)
    for i in range(10, 12):
        deliver(i, True)

    for h in range(2):
        for q in range(4):
            b_copy(h, q).wait_send()
            y_copy(h, q).wait_send()
        for t in range(2):
            v_copy(h, t, chunk(t)).wait_send()
            c_copy(h, t).wait_send()
    for late in range(2):
        for i in range(7):
            strip_copy(late, i).wait_send()
    for i in range(7):
        gather_copy(i).wait_send()
    for i in range(8):
        pass_copy(i, c).wait_send()
    for i in range(3):
        z_copy(i).wait_send()


    row_y, row_x = e // 4, e % 4
    dy, dx = (row_y + 2 - yhi) % 2, (row_x + 4 - x) % 4
    kind = dy * 4 + dx
    mirror_only = (kind == 3) | (kind == 5)
    straight_only = (kind == 0) | (kind == 1) | (kind == 7)

    def wait_straight():
        pltpu.make_async_copy(dd, dd, fr).wait()

    def wait_mirror():
        pltpu.make_async_copy(tt, tt, tr).wait()

    @pl.when(mirror_only)
    def _():
        wait_mirror()
        for h in range(2):
            out_ref[pl.ds(h * 128, 128)] = tt[h].T

    @pl.when(straight_only)
    def _():
        wait_straight()
        out_ref[...] = dd[...]

    @pl.when((kind == 2) | (kind == 4) | (kind == 6))
    def _():
        wait_straight()
        wait_mirror()
        for h in range(2):
            out_ref[pl.ds(h * 128, 128)] = dd[pl.ds(h * 128, 128)] + tt[h].T

    for i in range(12):
        deliver(i, False)


def per_device(grads, quads, volume, weight):
    f32, bf16 = jnp.float32, jnp.bfloat16
    dma = pltpu.SemaphoreType.DMA
    vmem = pl.BlockSpec(memory_space=pltpu.VMEM)
    return pl.pallas_call(
        kernel,
        out_shape=jax.ShapeDtypeStruct((256, 128), f32),
        in_specs=[vmem] * 4,
        out_specs=vmem,
        scratch_shapes=[
            pltpu.VMEM((2, 8, 384, 128), bf16),
            pltpu.VMEM((2, 8, 128), f32),
            pltpu.VMEM((2, 128, 128), f32),
            pltpu.VMEM((1024, 2048), bf16),
            pltpu.VMEM((1024, 2048), bf16),
            pltpu.VMEM((2, 128, 2048), bf16),
            pltpu.VMEM((2, 128, 2048), bf16),
            pltpu.VMEM((2, 128, 1024), bf16),
            pltpu.VMEM((2, 128, 2048), bf16),
            pltpu.VMEM((2, 128, 1024), bf16),
            pltpu.VMEM((2, 12, 128, 128), f32),
            pltpu.VMEM((12, 128, 128), f32),
            pltpu.VMEM((12, 2, 4, 16, 128), f32),
            pltpu.VMEM((8, 12, 16, 128), f32),
            pltpu.VMEM((12, 16, 128), f32),
            pltpu.VMEM((256, 128), f32),
            pltpu.VMEM((2, 128, 128), f32),
            pltpu.VMEM((4, 5, 2, 16, 128), f32),
            pltpu.VMEM((5, 2, 16, 128), f32),
            pltpu.VMEM((5, 16, 128), f32),
            dma((4,)), dma((4,)), dma((8,)), dma((8,)), dma((9,)), dma((9,)),
            dma((8,)), dma((8,)), dma((8,)), dma((8,)),
            dma((4,)), dma((4,)), dma((4,)), dma((4,)),
            dma((3,)), dma((3,)), dma((16,)), dma((16,)),
            dma((12,)), dma((12,)), dma, dma,
        ],
        compiler_params=pltpu.CompilerParams(
            collective_id=0, has_side_effects=True, vmem_limit_bytes=60000000
        ),
        name="hessian",
    )(grads, quads.T, volume.reshape(1, 128), weight.reshape(1, 4096))


def solution(mesh):
    placed = (P(None, "elec", "cell"), P("elec", None), P("cell"), P("elec"))
    return jax.shard_map(
        per_device, mesh=mesh, in_specs=placed, out_specs=P("elec", "cell"), check_vma=False
    )
```

```python
import functools

import jax
import jax.numpy as jnp
from jax import lax
from jax.experimental import pallas as pl
from jax.experimental.pallas import tpu as pltpu
from jax.sharding import PartitionSpec as P

MESH = pl.DeviceIdType.MESH
NT = (((1,), (1,)), ((), ()))
EARLY = [(0, 0), (0, 1), (1, 0), (2, 0), (3, 0)]
LATE = [(1, 1), (2, 1), (3, 1), (4, 0), (4, 1), (5, 0), (5, 1)]
BLOCKS = EARLY + LATE
GROUPS = [(0, 5), (5, 5), (10, 2)]
LATER = GROUPS[1:]
STEPS = [(1, 0), (0, 1), (0, 3), (0, 2), (1, 1), (1, 3), (1, 2)]
ROWS = [(0, 0), (0, 1), (0, 2), (1, 0), (1, 0), (1, 0)]
COLS = [(0, 0), (0, 0), (0, 0), (0, 0), (0, 1), (0, 2)]


def dot_nt(left, right):
    return lax.dot_general(left, right, NT, preferred_element_type=jnp.float32)


def kernel(
    g_in, q_in, v_in, w_in, out_ref,
    g_ref, q_ref, v_ref, w_ref, loads,
    gt, vol, vb, ms, mr, a, b, cc, y, v, sums, part, own, strips, fin, dd, tt,
    zparts, zsum, zback, zs, zr, gs, gr, ps, pr, bs, br, ys, yr, vs, vr, cs, cr, ks, kr, rs, rr, fs, ts, fr, tr,
):
    e = lax.axis_index("elec")
    cell = lax.axis_index("cell")
    ylo, z = e // 4, e % 4
    yhi, x, c = cell // 8, (cell // 2) % 4, cell % 2
    half_x = x // 2
    half_y = yhi

    def at(dy, dx, core):
        return (((yhi + dy) % 2) * 4 + (x + dx) % 4) * 2 + core

    def group(dy, dx):
        return ((yhi + dy) % 2) * 4 + (x + dx) % 4

    def send(src, dst, ssem, rsem, to):
        return pltpu.make_async_remote_copy(
            src, dst, ssem, rsem, device_id=to, device_id_type=MESH
        )

    def peer(i):
        dy, dz = STEPS[i]
        return ((ylo + dy) % 2) * 4 + (z + dz) % 4

    def source(i):
        dy, dz = STEPS[i]
        return ((ylo + dy) % 2) * 4 + (z + 4 - dz) % 4

    def piece(group_of, s):
        return gt.at[c, group_of, pl.ds(s * 192, 192)]

    arguments = [
        pltpu.make_async_copy(src, dst, loads.at[i])
        for i, (src, dst) in enumerate(
            ((g_in, g_ref), (v_in, v_ref), (q_in, q_ref), (w_in, w_ref))
        )
    ]
    for load in arguments:
        load.start()
    barrier = pltpu.get_barrier_semaphore()
    partner = (e, at(0, 0, 1 - c))
    near = [(peer(i), cell) for i in range(7)]
    near += [partner, (e, at(0, 1, c)), (e, at(0, 3, c)), (e, at(1, 0, c))]
    for device in near:
        pl.semaphore_signal(barrier, inc=1, device_id=device, device_id_type=MESH)

    for load in arguments[:2]:
        load.wait()
    for k in range(3):
        turned = g_ref[k].T
        for s in range(2):
            gt[c, e, pl.ds(s * 192 + k * 64, 64), :] = turned[s * 64 : s * 64 + 64]
    vol[c] = jnp.broadcast_to(v_ref[...], (8, 128))
    pl.semaphore_wait(barrier, len(near))

    def gather_copy(s, i):
        if i < 4 or s == 0:
            group_of, there = e, peer(i)
        elif i < 6:
            group_of, there = peer(0), ylo * 4 + peer(i) % 4
        else:
            group_of, there = ylo * 4 + (z + 2) % 4, peer(0)
        part_of = piece(group_of, s)
        return send(part_of, part_of, gs.at[s * 7 + i], gr.at[s * 7 + i], (there, cell))

    def pass_copy(s, i, core):
        group_of = e if i == 7 else source(i)
        part_of = gt.at[core, group_of, pl.ds(s * 192, 192)]
        return send(part_of, part_of, ps.at[s * 8 + i], pr.at[s * 8 + i], partner)

    def start_gather(s):
        for i in range(4 if s else 7):
            gather_copy(s, i).start()
        pass_copy(s, 7, c).start()

    def relay_y(s):
        gather_copy(s, 0).wait_recv()
        for i in range(4, 6):
            gather_copy(s, i).start()

    def relay_z(s):
        gather_copy(s, 3).wait_recv()
        gather_copy(s, 6).start()

    def pass_on(s):
        for i in range(7):
            if s == 0 or i not in (0, 3):
                gather_copy(s, i).wait_recv()
            pass_copy(s, i, c).start()

    def wait_passed(s):
        for i in range(8):
            pass_copy(s, i, 1 - c).wait_recv()

    def on_core(core, *steps):
        @pl.when(c == core)
        def _():
            for step, s in steps:
                step(s)

    on_core(0, (start_gather, 0))
    volume_copy = send(vol.at[c], vol.at[c], ps.at[16], pr.at[16], partner)
    volume_copy.start()

    for load in arguments[2:]:
        load.wait()
    base = pl.multiple_of(c * 2048, 2048)
    electrodes = [q_ref[pl.ds(k, 1), pl.ds(base, 2048)] for k in range(4)]

    def maps(row, carry):
        first = pl.multiple_of(row * 16, 16)
        label = lax.broadcasted_iota(jnp.int32, (16, 2048), 0) + first
        one = jnp.float32(1)
        ms[pl.ds(first, 16), :] = jnp.where(
            label == electrodes[0], one, jnp.where(label == electrodes[1], -one, 0.0)
        ).astype(jnp.bfloat16)
        mr[pl.ds(first, 16), :] = jnp.where(
            label == electrodes[2], one, jnp.where(label == electrodes[3], -one, 0.0)
        ).astype(jnp.bfloat16)
        return carry

    lax.fori_loop(0, 20, maps, 0)
    on_core(0, (start_gather, 1))
    lax.fori_loop(20, 40, maps, 0)
    on_core(0, (relay_y, 1))
    lax.fori_loop(40, 64, maps, 0)
    on_core(1, (start_gather, 0))
    volume_copy.wait()
    for h in range(2):
        vb[h] = jnp.broadcast_to(vol[h, 0:1, :], (128, 128)).T
    on_core(1, (start_gather, 1))
    on_core(0, (pass_on, 0), (relay_z, 1))
    on_core(1, (relay_y, 1), (wait_passed, 0))

    to_b = (e, at(0, 3, c))
    to_v = (e, at(0, 1, c))
    to_y = (e, at(1, 0, c))

    def columns(q, width=512):
        return pl.ds(pl.multiple_of(q * width, width), width)

    def span(h, s):
        return (pl.ds(s * 64, 64) if h == 0 else pl.ds(0, 128)), (s if h == 0 else 2)

    def b_copy(h, q, s=0):
        rows, slot = span(h, s)
        sem = slot * 4 + q
        return send(a.at[h, rows, columns(q)], b.at[h, rows, columns(q)], bs.at[sem], br.at[sem], to_b)

    def y_copy(h, q, s=0):
        rows, slot = span(h, s)
        sem = slot * 4 + q
        return send(a.at[h, rows, columns(q)], y.at[h, rows, columns(q)], ys.at[sem], yr.at[sem], to_y)

    def v_copy(h, t, q, s=0):
        rows, slot = span(h, s)
        sem = slot * 2 + t
        return send(a.at[h, rows, columns(q)], v.at[h, rows, columns(t)], vs.at[sem], vr.at[sem], to_v)

    def c_copy(h, t, s=0):
        rows, slot = span(h, s)
        sem = slot * 2 + t
        return send(v.at[h, rows, columns(t)], cc.at[h, rows, columns(t)], cs.at[sem], cr.at[sem], to_v)

    def chunk(t):
        return (t + 2 * (1 - half_x)) % 4

    def sensitivities(h, parts, t):
        q = chunk(t)
        cols = columns(q)
        first, last = parts[0] * 192, parts[-1] * 192 + 192
        field = jnp.concatenate([gt[h, i, first:last] for i in range(8)], axis=1)
        sources = jnp.dot(field, ms[:, cols], preferred_element_type=jnp.float32)
        receivers = jnp.dot(field, mr[:, cols], preferred_element_type=jnp.float32)
        gain = w_ref[:, pl.ds(pl.multiple_of(base + q * 512, 512), 512)]
        for s in parts:
            low = s * 192 - first
            dots = (
                sources[low : low + 64] * receivers[low : low + 64]
                + sources[low + 64 : low + 128] * receivers[low + 64 : low + 128]
                + sources[low + 128 : low + 192] * receivers[low + 128 : low + 192]
            )
            volumes = jnp.concatenate([vb[h, s * 64 : s * 64 + 64]] * 4, axis=1)
            a[h, s * 64 : s * 64 + 64, cols] = (gain * -(volumes * dots)).astype(jnp.bfloat16)
        if h == 0 and t < 2:
            v_copy(h, t, q, parts[0]).start()
        b_copy(h, q, parts[0]).start()
        y_copy(h, q, parts[0]).start()

    def forward(s, t):
        v_copy(0, t, chunk(t), s).wait_recv()
        c_copy(0, t, s).start()

    for t in range(4):
        sensitivities(0, [0], t)
        if t == 0:
            on_core(0, (pass_on, 1))
        if t == 1:
            on_core(1, (relay_z, 1))
    on_core(1, (wait_passed, 1))
    for t in range(4):
        sensitivities(0, [1], t)
        if t % 2:
            forward(0, t // 2)
    on_core(1, (pass_on, 0), (pass_on, 1))
    on_core(0, (wait_passed, 0), (wait_passed, 1))
    for t in range(4):
        sensitivities(1, [0, 1], t)
        if t % 2:
            forward(1, t // 2)

    def put(block, value):
        sums[0, block] = value[:, 0:128]
        sums[1, block] = value[:, 128:256]

    def a_part(half=None):
        if half is None:
            return a[...].reshape(256, 2048)
        return a[:, :, columns(half, 1024)].reshape(256, 1024)

    for t in range(2):
        v_copy(1, t, chunk(t)).start()
    whole = dot_nt(a_part(), a_part())
    put(0, whole[0:128])
    put(1, whole[128:256])

    def arrive(h):
        for s in range(2 - h):
            for q in range(4):
                b_copy(h, q, s).wait_recv()
                y_copy(h, q, s).wait_recv()
            for t in range(2):
                c_copy(h, t, s).wait_recv()

    def border(h, first):
        put(first, dot_nt(b[h], a_part()))
        put(first + 1, dot_nt(cc[h], a_part(half_x)))
        put(first + 2, dot_nt(y[h, :, columns(half_y, 1024)], a_part(half_y)))

    def core_copy(group_of):
        first, count = GROUPS[group_of]
        blocks = pl.ds(first, count)
        return send(
            sums.at[1 - c, blocks], part.at[blocks], ks.at[group_of], kr.at[group_of], partner
        )

    def add_cores(group_of):
        core_copy(group_of).wait()
        first, count = GROUPS[group_of]
        for i in range(first, first + count):
            own[i] = (sums[c, i] + part[i]).reshape(2, 4, 16, 128)

    def z_copy(i, receive=False):
        dz = (1, 3, 2)[i]
        there = (z + 4 - dz) % 4 if receive else (z + dz) % 4
        row = there if receive else z
        return send(
            own.at[pl.ds(0, 5), :, there], zparts.at[row], zs.at[i], zr.at[i],
            (ylo * 4 + there, cell),
        )

    def y_fold():
        return send(zsum.at[:, 1 - ylo], zback, zs.at[3], zr.at[3], ((1 - ylo) * 4 + z, cell))

    def fold_early():
        for i in range(3):
            z_copy(i, True).wait_recv()
        total = own[0:5, :, z]
        for i in range(3):
            total = total + zparts[(z + 4 - (1, 3, 2)[i]) % 4]
        zsum[...] = total
        y_fold().start()

    def finish_early():
        y_fold().wait()
        fin[0:5] = (zsum[:, ylo] + zback[...]) * jnp.float32(1.0 / 32768)

    def strip_copy(late, i, receive=False):
        first, count = LATER[late]
        blocks = pl.ds(first, count)
        if receive:
            there, slot = source(i), source(i)
        else:
            there, slot = peer(i), e
        return send(
            own.at[blocks, there // 4, there % 4], strips.at[slot, blocks],
            rs.at[late * 8 + i], rr.at[late * 8 + i], (there, cell),
        )

    def scatter(late):
        for i in range(7):
            strip_copy(late, i).start()

    def gather_strips(late):
        first, count = LATER[late]
        last = first + count
        total = own[first:last, ylo, z]
        for i in range(7):
            strip_copy(late, i, True).wait_recv()
        for i in range(7):
            total = total + strips[source(i), first:last]
        fin[first:last] = total * jnp.float32(1.0 / 32768)

    def deliver(i, start):
        k, r = BLOCKS[i]
        row_half = r
        offset = pl.multiple_of(e * 16, 16)
        landing = dd.at[pl.ds(pl.multiple_of(row_half * 128 + e * 16, 16), 16)]
        row_group, col_group = group(*ROWS[k]), group(*COLS[k])
        copy = send(fin.at[i], landing, fs.at[i], fr, (row_group, col_group * 2 + c))
        if COLS[k] == (0, 0):
            @pl.when(row_group == e)
            def _():
                if start:
                    pltpu.make_async_copy(fin.at[i], landing, fr).start()

            @pl.when(row_group != e)
            def _():
                if start:
                    copy.start()
                else:
                    copy.wait_send()
        elif start:
            copy.start()
        else:
            copy.wait_send()
        if k:
            mirror = send(
                fin.at[i], tt.at[c, pl.ds(offset, 16)], ts.at[i], tr,
                (col_group, row_group * 2 + row_half),
            )
            if start:
                mirror.start()
            else:
                mirror.wait_send()

    arrive(0)
    border(0, 2)
    core_copy(0).start()
    for t in range(2):
        v_copy(1, t, chunk(t)).wait_recv()
        c_copy(1, t).start()
    add_cores(0)
    for i in range(3):
        z_copy(i).start()
    fold_early()

    def halves(ref, half):
        return ref[:, :, columns(half, 1024)].reshape(256, 1024)

    for q in range(2):
        b_copy(1, q).wait_recv()
        y_copy(1, q).wait_recv()
    border_b = dot_nt(b[1, :, 0:1024], a_part(0))
    corner_b = dot_nt(halves(y, 0), halves(b, 0))
    for q in range(2, 4):
        b_copy(1, q).wait_recv()
        y_copy(1, q).wait_recv()
    put(5, border_b + dot_nt(b[1, :, 1024:2048], a_part(1)))
    put(7, dot_nt(y[1, :, columns(half_y, 1024)], a_part(half_y)))
    whole = corner_b + dot_nt(halves(y, 1), halves(b, 1))
    put(8, whole[0:128])
    put(9, whole[128:256])
    for t in range(2):
        c_copy(1, t).wait_recv()
    put(6, dot_nt(cc[1], a_part(half_x)))
    core_copy(1).start()
    whole = dot_nt(halves(y, half_x), cc[...].reshape(256, 1024))
    put(10, whole[0:128])
    put(11, whole[128:256])
    core_copy(2).start()
    add_cores(1)
    scatter(0)
    add_cores(2)
    scatter(1)
    finish_early()
    for i in range(5):
        deliver(i, True)
    gather_strips(0)
    for i in range(5, 10):
        deliver(i, True)
    gather_strips(1)
    for i in range(10, 12):
        deliver(i, True)

    for h, s in ((0, 0), (0, 1), (1, 0)):
        for q in range(4):
            b_copy(h, q, s).wait_send()
            y_copy(h, q, s).wait_send()
        for t in range(2):
            v_copy(h, t, chunk(t), s).wait_send()
            c_copy(h, t, s).wait_send()
    for late in range(2):
        for i in range(7):
            strip_copy(late, i).wait_send()
    for s in range(2):
        for i in range(7):
            gather_copy(s, i).wait_send()
        for i in range(8):
            pass_copy(s, i, c).wait_send()
    for i in range(3):
        z_copy(i).wait_send()


    row_y, row_x = e // 4, e % 4
    dy, dx = (row_y + 2 - yhi) % 2, (row_x + 4 - x) % 4
    kind = dy * 4 + dx
    mirror_only = (kind == 3) | (kind == 5)
    straight_only = (kind == 0) | (kind == 1) | (kind == 7)

    def wait_straight():
        pltpu.make_async_copy(dd, dd, fr).wait()

    def wait_mirror():
        pltpu.make_async_copy(tt, tt, tr).wait()

    @pl.when(mirror_only)
    def _():
        wait_mirror()
        for h in range(2):
            out_ref[pl.ds(h * 128, 128)] = tt[h].T

    @pl.when(straight_only)
    def _():
        wait_straight()
        out_ref[...] = dd[...]

    @pl.when((kind == 2) | (kind == 4) | (kind == 6))
    def _():
        wait_straight()
        wait_mirror()
        for h in range(2):
            out_ref[pl.ds(h * 128, 128)] = dd[pl.ds(h * 128, 128)] + tt[h].T

    for i in range(12):
        deliver(i, False)


def per_device(grads, quads, volume, weight):
    f32, bf16 = jnp.float32, jnp.bfloat16
    dma = pltpu.SemaphoreType.DMA
    vmem = pl.BlockSpec(memory_space=pltpu.VMEM)
    return pl.pallas_call(
        kernel,
        out_shape=pltpu.VMEM((256, 128), f32),
        in_specs=[pl.BlockSpec(memory_space=pl.ANY)] * 4,
        out_specs=vmem,
        scratch_shapes=[
            pltpu.VMEM((3, 128, 128), bf16),
            pltpu.VMEM((4, 4096), jnp.int32),
            pltpu.VMEM((1, 128), f32),
            pltpu.VMEM((1, 4096), f32),
            dma((4,)),
            pltpu.VMEM((2, 8, 384, 128), bf16),
            pltpu.VMEM((2, 8, 128), f32),
            pltpu.VMEM((2, 128, 128), f32),
            pltpu.VMEM((1024, 2048), bf16),
            pltpu.VMEM((1024, 2048), bf16),
            pltpu.VMEM((2, 128, 2048), bf16),
            pltpu.VMEM((2, 128, 2048), bf16),
            pltpu.VMEM((2, 128, 1024), bf16),
            pltpu.VMEM((2, 128, 2048), bf16),
            pltpu.VMEM((2, 128, 1024), bf16),
            pltpu.VMEM((2, 12, 128, 128), f32),
            pltpu.VMEM((12, 128, 128), f32),
            pltpu.VMEM((12, 2, 4, 16, 128), f32),
            pltpu.VMEM((8, 12, 16, 128), f32),
            pltpu.VMEM((12, 16, 128), f32),
            pltpu.VMEM((256, 128), f32),
            pltpu.VMEM((2, 128, 128), f32),
            pltpu.VMEM((4, 5, 2, 16, 128), f32),
            pltpu.VMEM((5, 2, 16, 128), f32),
            pltpu.VMEM((5, 16, 128), f32),
            dma((4,)), dma((4,)), dma((14,)), dma((14,)), dma((17,)), dma((17,)),
            dma((12,)), dma((12,)), dma((12,)), dma((12,)),
            dma((6,)), dma((6,)), dma((6,)), dma((6,)),
            dma((3,)), dma((3,)), dma((16,)), dma((16,)),
            dma((12,)), dma((12,)), dma, dma,
        ],
        compiler_params=pltpu.CompilerParams(
            collective_id=0, has_side_effects=True, vmem_limit_bytes=60000000
        ),
        name="hessian",
    )(grads, quads.T, volume.reshape(1, 128), weight.reshape(1, 4096))


def solution(mesh):
    placed = (P(None, "elec", "cell"), P("elec", None), P("cell"), P("elec"))
    return jax.shard_map(
        per_device, mesh=mesh, in_specs=placed, out_specs=P("elec", "cell"), check_vma=False
    )
```

```python
import functools

import jax
import jax.numpy as jnp
from jax import lax
from jax.experimental import pallas as pl
from jax.experimental.pallas import tpu as pltpu
from jax.sharding import PartitionSpec as P

MESH = pl.DeviceIdType.MESH
NT = (((1,), (1,)), ((), ()))
EARLY = [(0, 0), (0, 1), (1, 0), (2, 0), (3, 0)]
LATE = [(1, 1), (2, 1), (3, 1), (4, 0), (4, 1), (5, 0), (5, 1)]
BLOCKS = EARLY + LATE
GROUPS = [(0, 5), (5, 3), (8, 2), (10, 2)]
LATER = GROUPS[1:]
STEPS = [(1, 0), (0, 1), (0, 3), (0, 2), (1, 1), (1, 3), (1, 2)]
ROWS = [(0, 0), (0, 1), (0, 2), (1, 0), (1, 0), (1, 0)]
COLS = [(0, 0), (0, 0), (0, 0), (0, 0), (0, 1), (0, 2)]


def dot_nt(left, right):
    return lax.dot_general(left, right, NT, preferred_element_type=jnp.float32)


def kernel(
    g_in, q_in, v_in, w_in, out_ref,
    g_ref, q_ref, v_ref, w_ref, loads,
    gt, vol, vb, ms, mr, a, b, cc, y, v, sums, part, own, strips, fin, dd, tt,
    zparts, zsum, zback, zs, zr, gs, gr, ps, pr, bs, br, ys, yr, vs, vr, cs, cr, ks, kr, rs, rr, fs, ts, fr, tr,
):
    e = lax.axis_index("elec")
    cell = lax.axis_index("cell")
    ylo, z = e // 4, e % 4
    yhi, x, c = cell // 8, (cell // 2) % 4, cell % 2
    half_x = x // 2
    half_y = yhi

    def at(dy, dx, core):
        return (((yhi + dy) % 2) * 4 + (x + dx) % 4) * 2 + core

    def group(dy, dx):
        return ((yhi + dy) % 2) * 4 + (x + dx) % 4

    def send(src, dst, ssem, rsem, to):
        return pltpu.make_async_remote_copy(
            src, dst, ssem, rsem, device_id=to, device_id_type=MESH
        )

    def peer(i):
        dy, dz = STEPS[i]
        return ((ylo + dy) % 2) * 4 + (z + dz) % 4

    def source(i):
        dy, dz = STEPS[i]
        return ((ylo + dy) % 2) * 4 + (z + 4 - dz) % 4

    def piece(group_of, s):
        return gt.at[c, group_of, pl.ds(s * 192, 192)]

    arguments = [
        pltpu.make_async_copy(src, dst, loads.at[i])
        for i, (src, dst) in enumerate(
            ((g_in, g_ref), (v_in, v_ref), (q_in, q_ref), (w_in, w_ref))
        )
    ]
    for load in arguments:
        load.start()
    barrier = pltpu.get_barrier_semaphore()
    partner = (e, at(0, 0, 1 - c))
    near = [(peer(i), cell) for i in range(7)]
    near += [partner, (e, at(0, 1, c)), (e, at(0, 3, c)), (e, at(1, 0, c))]
    for device in near:
        pl.semaphore_signal(barrier, inc=1, device_id=device, device_id_type=MESH)

    for load in arguments[:2]:
        load.wait()
    for k in range(3):
        turned = g_ref[k].T
        for s in range(2):
            gt[c, e, pl.ds(s * 192 + k * 64, 64), :] = turned[s * 64 : s * 64 + 64]
    vol[c] = jnp.broadcast_to(v_ref[...], (8, 128))
    pl.semaphore_wait(barrier, len(near))

    def gather_copy(s, i):
        if i < 4 or s == 0:
            group_of, there = e, peer(i)
        elif i < 6:
            group_of, there = peer(0), ylo * 4 + peer(i) % 4
        else:
            group_of, there = ylo * 4 + (z + 2) % 4, peer(0)
        part_of = piece(group_of, s)
        return send(part_of, part_of, gs.at[s * 7 + i], gr.at[s * 7 + i], (there, cell))

    def pass_copy(s, i, core):
        group_of = e if i == 7 else source(i)
        part_of = gt.at[core, group_of, pl.ds(s * 192, 192)]
        return send(part_of, part_of, ps.at[s * 8 + i], pr.at[s * 8 + i], partner)

    def start_gather(s):
        for i in range(4 if s else 7):
            gather_copy(s, i).start()
        pass_copy(s, 7, c).start()

    def relay_y(s):
        gather_copy(s, 0).wait_recv()
        for i in range(4, 6):
            gather_copy(s, i).start()

    def relay_z(s):
        gather_copy(s, 3).wait_recv()
        gather_copy(s, 6).start()

    def pass_on(s):
        for i in range(7):
            if s == 0 or i not in (0, 3):
                gather_copy(s, i).wait_recv()
            pass_copy(s, i, c).start()

    def wait_passed(s):
        for i in range(8):
            pass_copy(s, i, 1 - c).wait_recv()

    def on_core(core, *steps):
        @pl.when(c == core)
        def _():
            for step, s in steps:
                step(s)

    on_core(0, (start_gather, 0))
    volume_copy = send(vol.at[c], vol.at[c], ps.at[16], pr.at[16], partner)
    volume_copy.start()

    for load in arguments[2:]:
        load.wait()
    base = pl.multiple_of(c * 2048, 2048)
    electrodes = [q_ref[pl.ds(k, 1), pl.ds(base, 2048)] for k in range(4)]

    def maps(row, carry):
        first = pl.multiple_of(row * 16, 16)
        label = lax.broadcasted_iota(jnp.int32, (16, 2048), 0) + first
        one = jnp.float32(1)
        ms[pl.ds(first, 16), :] = jnp.where(
            label == electrodes[0], one, jnp.where(label == electrodes[1], -one, 0.0)
        ).astype(jnp.bfloat16)
        mr[pl.ds(first, 16), :] = jnp.where(
            label == electrodes[2], one, jnp.where(label == electrodes[3], -one, 0.0)
        ).astype(jnp.bfloat16)
        return carry

    lax.fori_loop(0, 20, maps, 0)
    on_core(0, (start_gather, 1))
    lax.fori_loop(20, 40, maps, 0)
    on_core(0, (relay_y, 1))
    lax.fori_loop(40, 64, maps, 0)
    on_core(1, (start_gather, 0))
    volume_copy.wait()
    for h in range(2):
        vb[h] = jnp.broadcast_to(vol[h, 0:1, :], (128, 128)).T
    on_core(1, (start_gather, 1))
    on_core(0, (pass_on, 0), (relay_z, 1))
    on_core(1, (relay_y, 1), (wait_passed, 0))

    to_b = (e, at(0, 3, c))
    to_v = (e, at(0, 1, c))
    to_y = (e, at(1, 0, c))

    def columns(q, width=512):
        return pl.ds(pl.multiple_of(q * width, width), width)

    def span(h, s):
        return (pl.ds(s * 64, 64) if h == 0 else pl.ds(0, 128)), (s if h == 0 else 2)

    def b_copy(h, q, s=0):
        rows, slot = span(h, s)
        sem = slot * 4 + q
        return send(a.at[h, rows, columns(q)], b.at[h, rows, columns(q)], bs.at[sem], br.at[sem], to_b)

    def y_copy(h, q, s=0):
        rows, slot = span(h, s)
        sem = slot * 4 + q
        return send(a.at[h, rows, columns(q)], y.at[h, rows, columns(q)], ys.at[sem], yr.at[sem], to_y)

    def v_copy(h, t, q, s=0):
        rows, slot = span(h, s)
        sem = slot * 2 + t
        return send(a.at[h, rows, columns(q)], v.at[h, rows, columns(t)], vs.at[sem], vr.at[sem], to_v)

    def c_copy(h, t, s=0):
        rows, slot = span(h, s)
        sem = slot * 2 + t
        return send(v.at[h, rows, columns(t)], cc.at[h, rows, columns(t)], cs.at[sem], cr.at[sem], to_v)

    def chunk(t):
        return (t + 2 * (1 - half_x)) % 4

    def sensitivities(h, parts, t):
        q = chunk(t)
        cols = columns(q)
        first, last = parts[0] * 192, parts[-1] * 192 + 192
        field = jnp.concatenate([gt[h, i, first:last] for i in range(8)], axis=1)
        sources = jnp.dot(field, ms[:, cols], preferred_element_type=jnp.float32)
        receivers = jnp.dot(field, mr[:, cols], preferred_element_type=jnp.float32)
        gain = w_ref[:, pl.ds(pl.multiple_of(base + q * 512, 512), 512)]
        for s in parts:
            low = s * 192 - first
            dots = (
                sources[low : low + 64] * receivers[low : low + 64]
                + sources[low + 64 : low + 128] * receivers[low + 64 : low + 128]
                + sources[low + 128 : low + 192] * receivers[low + 128 : low + 192]
            )
            volumes = jnp.concatenate([vb[h, s * 64 : s * 64 + 64]] * 4, axis=1)
            a[h, s * 64 : s * 64 + 64, cols] = (gain * -(volumes * dots)).astype(jnp.bfloat16)
        if h == 0 and t < 2:
            v_copy(h, t, q, parts[0]).start()
        b_copy(h, q, parts[0]).start()
        y_copy(h, q, parts[0]).start()

    def forward(s, t):
        v_copy(0, t, chunk(t), s).wait_recv()
        c_copy(0, t, s).start()

    for t in range(4):
        sensitivities(0, [0], t)
        if t == 0:
            on_core(0, (pass_on, 1))
        if t == 1:
            on_core(1, (relay_z, 1))
    on_core(1, (wait_passed, 1))
    for t in range(4):
        sensitivities(0, [1], t)
        if t % 2:
            forward(0, t // 2)
    on_core(1, (pass_on, 0), (pass_on, 1))
    on_core(0, (wait_passed, 0), (wait_passed, 1))
    for t in range(4):
        sensitivities(1, [0, 1], t)
        if t % 2:
            forward(1, t // 2)

    def put(block, value):
        sums[0, block] = value[:, 0:128]
        sums[1, block] = value[:, 128:256]

    def a_part(half=None):
        if half is None:
            return a[...].reshape(256, 2048)
        return a[:, :, columns(half, 1024)].reshape(256, 1024)

    for t in range(2):
        v_copy(1, t, chunk(t)).start()
    whole = dot_nt(a_part(), a_part())
    put(0, whole[0:128])
    put(1, whole[128:256])

    def arrive(h):
        for s in range(2 - h):
            for q in range(4):
                b_copy(h, q, s).wait_recv()
                y_copy(h, q, s).wait_recv()
            for t in range(2):
                c_copy(h, t, s).wait_recv()

    def border(h, first):
        put(first, dot_nt(b[h], a_part()))
        put(first + 1, dot_nt(cc[h], a_part(half_x)))
        put(first + 2, dot_nt(y[h, :, columns(half_y, 1024)], a_part(half_y)))

    def core_copy(group_of):
        first, count = GROUPS[group_of]
        blocks = pl.ds(first, count)
        return send(
            sums.at[1 - c, blocks], part.at[blocks], ks.at[group_of], kr.at[group_of], partner
        )

    def add_cores(group_of):
        core_copy(group_of).wait()
        first, count = GROUPS[group_of]
        for i in range(first, first + count):
            own[i] = (sums[c, i] + part[i]).reshape(2, 4, 16, 128)

    def z_copy(i, receive=False):
        dz = (1, 3, 2)[i]
        there = (z + 4 - dz) % 4 if receive else (z + dz) % 4
        row = there if receive else z
        return send(
            own.at[pl.ds(0, 5), :, there], zparts.at[row], zs.at[i], zr.at[i],
            (ylo * 4 + there, cell),
        )

    def y_fold():
        return send(zsum.at[:, 1 - ylo], zback, zs.at[3], zr.at[3], ((1 - ylo) * 4 + z, cell))

    def fold_early():
        for i in range(3):
            z_copy(i, True).wait_recv()
        total = own[0:5, :, z]
        for i in range(3):
            total = total + zparts[(z + 4 - (1, 3, 2)[i]) % 4]
        zsum[...] = total
        y_fold().start()

    def finish_early():
        y_fold().wait()
        fin[0:5] = (zsum[:, ylo] + zback[...]) * jnp.float32(1.0 / 32768)

    def strip_copy(late, i, receive=False):
        first, count = LATER[late]
        blocks = pl.ds(first, count)
        if receive:
            there, slot = source(i), source(i)
        else:
            there, slot = peer(i), e
        return send(
            own.at[blocks, there // 4, there % 4], strips.at[slot, blocks],
            rs.at[late * 8 + i], rr.at[late * 8 + i], (there, cell),
        )

    def scatter(late):
        for i in (6, 4, 5, 3, 0, 1, 2):
            strip_copy(late, i).start()

    def gather_strips(late):
        first, count = LATER[late]
        last = first + count
        total = own[first:last, ylo, z]
        for i in range(7):
            strip_copy(late, i, True).wait_recv()
        for i in range(7):
            total = total + strips[source(i), first:last]
        fin[first:last] = total * jnp.float32(1.0 / 32768)

    def deliver(i, start):
        k, r = BLOCKS[i]
        row_half = r
        offset = pl.multiple_of(e * 16, 16)
        landing = dd.at[pl.ds(pl.multiple_of(row_half * 128 + e * 16, 16), 16)]
        row_group, col_group = group(*ROWS[k]), group(*COLS[k])
        copy = send(fin.at[i], landing, fs.at[i], fr, (row_group, col_group * 2 + c))
        if COLS[k] == (0, 0):
            @pl.when(row_group == e)
            def _():
                if start:
                    pltpu.make_async_copy(fin.at[i], landing, fr).start()

            @pl.when(row_group != e)
            def _():
                if start:
                    copy.start()
                else:
                    copy.wait_send()
        elif start:
            copy.start()
        else:
            copy.wait_send()
        if k:
            mirror = send(
                fin.at[i], tt.at[c, pl.ds(offset, 16)], ts.at[i], tr,
                (col_group, row_group * 2 + row_half),
            )
            if start:
                mirror.start()
            else:
                mirror.wait_send()

    arrive(0)
    border(0, 2)
    core_copy(0).start()
    for t in range(2):
        v_copy(1, t, chunk(t)).wait_recv()
        c_copy(1, t).start()
    add_cores(0)
    for i in range(3):
        z_copy(i).start()
    fold_early()

    def halves(ref, half):
        return ref[:, :, columns(half, 1024)].reshape(256, 1024)

    for q in range(2):
        b_copy(1, q).wait_recv()
        y_copy(1, q).wait_recv()
    border_b = dot_nt(b[1, :, 0:1024], a_part(0))
    corner_b = dot_nt(halves(y, 0), halves(b, 0))
    for q in range(2, 4):
        b_copy(1, q).wait_recv()
        y_copy(1, q).wait_recv()
    put(5, border_b + dot_nt(b[1, :, 1024:2048], a_part(1)))
    put(7, dot_nt(y[1, :, columns(half_y, 1024)], a_part(half_y)))
    for t in range(2):
        c_copy(1, t).wait_recv()
    put(6, dot_nt(cc[1], a_part(half_x)))
    core_copy(1).start()
    whole = corner_b + dot_nt(halves(y, 1), halves(b, 1))
    put(8, whole[0:128])
    put(9, whole[128:256])
    core_copy(2).start()
    whole = dot_nt(halves(y, half_x), cc[...].reshape(256, 1024))
    put(10, whole[0:128])
    put(11, whole[128:256])
    core_copy(3).start()
    for late in range(3):
        add_cores(late + 1)
        scatter(late)
    for late in range(3):
        gather_strips(late)
        if late == 0:
            finish_early()
            for i in range(5):
                deliver(i, True)
        first, count = LATER[late]
        for i in range(first, first + count):
            deliver(i, True)

    for h, s in ((0, 0), (0, 1), (1, 0)):
        for q in range(4):
            b_copy(h, q, s).wait_send()
            y_copy(h, q, s).wait_send()
        for t in range(2):
            v_copy(h, t, chunk(t), s).wait_send()
            c_copy(h, t, s).wait_send()
    for late in range(3):
        for i in range(7):
            strip_copy(late, i).wait_send()
    for s in range(2):
        for i in range(7):
            gather_copy(s, i).wait_send()
        for i in range(8):
            pass_copy(s, i, c).wait_send()
    for i in range(3):
        z_copy(i).wait_send()


    row_y, row_x = e // 4, e % 4
    dy, dx = (row_y + 2 - yhi) % 2, (row_x + 4 - x) % 4
    kind = dy * 4 + dx
    mirror_only = (kind == 3) | (kind == 5)
    straight_only = (kind == 0) | (kind == 1) | (kind == 7)

    def wait_straight():
        pltpu.make_async_copy(dd, dd, fr).wait()

    def wait_mirror():
        pltpu.make_async_copy(tt, tt, tr).wait()

    @pl.when(mirror_only)
    def _():
        wait_mirror()
        for h in range(2):
            out_ref[pl.ds(h * 128, 128)] = tt[h].T

    @pl.when(straight_only)
    def _():
        wait_straight()
        out_ref[...] = dd[...]

    @pl.when((kind == 2) | (kind == 4) | (kind == 6))
    def _():
        wait_straight()
        wait_mirror()
        for h in range(2):
            out_ref[pl.ds(h * 128, 128)] = dd[pl.ds(h * 128, 128)] + tt[h].T

    for i in range(12):
        deliver(i, False)


def per_device(grads, quads, volume, weight):
    f32, bf16 = jnp.float32, jnp.bfloat16
    dma = pltpu.SemaphoreType.DMA
    vmem = pl.BlockSpec(memory_space=pltpu.VMEM)
    return pl.pallas_call(
        kernel,
        out_shape=pltpu.VMEM((256, 128), f32),
        in_specs=[pl.BlockSpec(memory_space=pl.ANY)] * 4,
        out_specs=vmem,
        scratch_shapes=[
            pltpu.VMEM((3, 128, 128), bf16),
            pltpu.VMEM((4, 4096), jnp.int32),
            pltpu.VMEM((1, 128), f32),
            pltpu.VMEM((1, 4096), f32),
            dma((4,)),
            pltpu.VMEM((2, 8, 384, 128), bf16),
            pltpu.VMEM((2, 8, 128), f32),
            pltpu.VMEM((2, 128, 128), f32),
            pltpu.VMEM((1024, 2048), bf16),
            pltpu.VMEM((1024, 2048), bf16),
            pltpu.VMEM((2, 128, 2048), bf16),
            pltpu.VMEM((2, 128, 2048), bf16),
            pltpu.VMEM((2, 128, 1024), bf16),
            pltpu.VMEM((2, 128, 2048), bf16),
            pltpu.VMEM((2, 128, 1024), bf16),
            pltpu.VMEM((2, 12, 128, 128), f32),
            pltpu.VMEM((12, 128, 128), f32),
            pltpu.VMEM((12, 2, 4, 16, 128), f32),
            pltpu.VMEM((8, 12, 16, 128), f32),
            pltpu.VMEM((12, 16, 128), f32),
            pltpu.VMEM((256, 128), f32),
            pltpu.VMEM((2, 128, 128), f32),
            pltpu.VMEM((4, 5, 2, 16, 128), f32),
            pltpu.VMEM((5, 2, 16, 128), f32),
            pltpu.VMEM((5, 16, 128), f32),
            dma((4,)), dma((4,)), dma((14,)), dma((14,)), dma((17,)), dma((17,)),
            dma((12,)), dma((12,)), dma((12,)), dma((12,)),
            dma((6,)), dma((6,)), dma((6,)), dma((6,)),
            dma((4,)), dma((4,)), dma((24,)), dma((24,)),
            dma((12,)), dma((12,)), dma, dma,
        ],
        compiler_params=pltpu.CompilerParams(
            collective_id=0, has_side_effects=True, vmem_limit_bytes=60000000
        ),
        name="hessian",
    )(grads, quads.T, volume.reshape(1, 128), weight.reshape(1, 4096))


def solution(mesh):
    placed = (P(None, "elec", "cell"), P("elec", None), P("cell"), P("elec"))
    return jax.shard_map(
        per_device, mesh=mesh, in_specs=placed, out_specs=P("elec", "cell"), check_vma=False
    )
```

```python
import functools

import jax
import jax.numpy as jnp
from jax import lax
from jax.experimental import pallas as pl
from jax.experimental.pallas import tpu as pltpu
from jax.sharding import PartitionSpec as P

MESH = pl.DeviceIdType.MESH
NT = (((1,), (1,)), ((), ()))
EARLY = [(0, 0), (0, 1), (1, 0), (2, 0), (3, 0)]
LATE = [(1, 1), (2, 1), (3, 1), (4, 0), (4, 1), (5, 0), (5, 1)]
BLOCKS = EARLY + LATE
GROUPS = [(0, 5), (5, 3), (8, 2), (10, 2)]
LATER = GROUPS[1:]
STEPS = [(1, 0), (0, 1), (0, 3), (0, 2), (1, 1), (1, 3), (1, 2)]
ROWS = [(0, 0), (0, 1), (0, 2), (1, 0), (1, 0), (1, 0)]
COLS = [(0, 0), (0, 0), (0, 0), (0, 0), (0, 1), (0, 2)]


def dot_nt(left, right):
    return lax.dot_general(left, right, NT, preferred_element_type=jnp.float32)


def kernel(
    g_in, q_in, v_in, w_in, out_ref,
    g_ref, q_ref, v_ref, w_ref, loads,
    gt, vol, vb, ms, mr, a, b, cc, y, v, sums, part, own, strips, fin, dd, tt,
    zparts, zsum, zback, zs, zr, gs, gr, ps, pr, bs, br, ys, yr, vs, vr, cs, cr, ks, kr, rs, rr, fs, ts, fr, tr,
):
    e = lax.axis_index("elec")
    cell = lax.axis_index("cell")
    ylo, z = e // 4, e % 4
    yhi, x, c = cell // 8, (cell // 2) % 4, cell % 2
    half_x = x // 2
    half_y = yhi

    def at(dy, dx, core):
        return (((yhi + dy) % 2) * 4 + (x + dx) % 4) * 2 + core

    def group(dy, dx):
        return ((yhi + dy) % 2) * 4 + (x + dx) % 4

    def send(src, dst, ssem, rsem, to):
        return pltpu.make_async_remote_copy(
            src, dst, ssem, rsem, device_id=to, device_id_type=MESH
        )

    def peer(i):
        dy, dz = STEPS[i]
        return ((ylo + dy) % 2) * 4 + (z + dz) % 4

    def source(i):
        dy, dz = STEPS[i]
        return ((ylo + dy) % 2) * 4 + (z + 4 - dz) % 4

    def piece(group_of, s):
        return gt.at[c, group_of, pl.ds(s * 192, 192)]

    arguments = [
        pltpu.make_async_copy(src, dst, loads.at[i])
        for i, (src, dst) in enumerate(
            ((g_in, g_ref), (v_in, v_ref), (q_in, q_ref), (w_in, w_ref))
        )
    ]
    for load in arguments:
        load.start()
    barrier = pltpu.get_barrier_semaphore()
    partner = (e, at(0, 0, 1 - c))
    near = [(peer(i), cell) for i in range(7)]
    near += [partner, (e, at(0, 1, c)), (e, at(0, 3, c)), (e, at(1, 0, c))]
    for device in near:
        pl.semaphore_signal(barrier, inc=1, device_id=device, device_id_type=MESH)

    for load in arguments[:2]:
        load.wait()
    for k in range(3):
        turned = g_ref[k].T
        for s in range(2):
            gt[c, e, pl.ds(s * 192 + k * 64, 64), :] = turned[s * 64 : s * 64 + 64]
    vol[c] = jnp.broadcast_to(v_ref[...], (8, 128))
    pl.semaphore_wait(barrier, len(near))

    def gather_copy(s, i):
        if i < 4 or s == 0:
            group_of, there = e, peer(i)
        elif i < 6:
            group_of, there = peer(0), ylo * 4 + peer(i) % 4
        else:
            group_of, there = ylo * 4 + (z + 2) % 4, peer(0)
        part_of = piece(group_of, s)
        return send(part_of, part_of, gs.at[s * 7 + i], gr.at[s * 7 + i], (there, cell))

    def pass_copy(s, i, core):
        group_of = e if i == 7 else source(i)
        part_of = gt.at[core, group_of, pl.ds(s * 192, 192)]
        return send(part_of, part_of, ps.at[s * 8 + i], pr.at[s * 8 + i], partner)

    def start_gather(s):
        for i in range(4 if s else 7):
            gather_copy(s, i).start()
        pass_copy(s, 7, c).start()

    def relay_y(s):
        gather_copy(s, 0).wait_recv()
        for i in range(4, 6):
            gather_copy(s, i).start()

    def relay_z(s):
        gather_copy(s, 3).wait_recv()
        gather_copy(s, 6).start()

    def pass_on(s):
        for i in range(7):
            if s == 0 or i not in (0, 3):
                gather_copy(s, i).wait_recv()
            pass_copy(s, i, c).start()

    def wait_passed(s):
        for i in range(8):
            pass_copy(s, i, 1 - c).wait_recv()

    def on_core(core, *steps):
        @pl.when(c == core)
        def _():
            for step, s in steps:
                step(s)

    on_core(0, (start_gather, 0))
    volume_copy = send(vol.at[c], vol.at[c], ps.at[16], pr.at[16], partner)
    volume_copy.start()

    for load in arguments[2:]:
        load.wait()
    base = pl.multiple_of(c * 2048, 2048)
    electrodes = [q_ref[pl.ds(k, 1), pl.ds(base, 2048)] for k in range(4)]

    def maps(row, carry):
        first = pl.multiple_of(row * 16, 16)
        label = lax.broadcasted_iota(jnp.int32, (16, 2048), 0) + first
        one = jnp.float32(1)
        ms[pl.ds(first, 16), :] = jnp.where(
            label == electrodes[0], one, jnp.where(label == electrodes[1], -one, 0.0)
        ).astype(jnp.bfloat16)
        mr[pl.ds(first, 16), :] = jnp.where(
            label == electrodes[2], one, jnp.where(label == electrodes[3], -one, 0.0)
        ).astype(jnp.bfloat16)
        return carry

    lax.fori_loop(0, 20, maps, 0)
    on_core(0, (start_gather, 1))
    lax.fori_loop(20, 40, maps, 0)
    on_core(0, (relay_y, 1))
    lax.fori_loop(40, 64, maps, 0)
    on_core(1, (start_gather, 0))
    volume_copy.wait()
    for h in range(2):
        vb[h] = jnp.broadcast_to(vol[h, 0:1, :], (128, 128)).T
    on_core(1, (start_gather, 1))
    on_core(0, (pass_on, 0), (relay_z, 1))
    on_core(1, (relay_y, 1), (wait_passed, 0))

    to_b = (e, at(0, 3, c))
    to_v = (e, at(0, 1, c))
    to_y = (e, at(1, 0, c))

    def columns(q, width=512):
        return pl.ds(pl.multiple_of(q * width, width), width)

    def span(h, s):
        return (pl.ds(s * 64, 64) if h == 0 else pl.ds(0, 128)), (s if h == 0 else 2)

    def b_copy(h, q, s=0):
        rows, slot = span(h, s)
        sem = slot * 4 + q
        return send(a.at[h, rows, columns(q)], b.at[h, rows, columns(q)], bs.at[sem], br.at[sem], to_b)

    def y_copy(h, q, s=0):
        rows, slot = span(h, s)
        sem = slot * 4 + q
        return send(a.at[h, rows, columns(q)], y.at[h, rows, columns(q)], ys.at[sem], yr.at[sem], to_y)

    def v_copy(h, t, q, s=0):
        rows, slot = span(h, s)
        sem = slot * 2 + t
        return send(a.at[h, rows, columns(q)], v.at[h, rows, columns(t)], vs.at[sem], vr.at[sem], to_v)

    def c_copy(h, t, s=0):
        rows, slot = span(h, s)
        sem = slot * 2 + t
        return send(v.at[h, rows, columns(t)], cc.at[h, rows, columns(t)], cs.at[sem], cr.at[sem], to_v)

    def chunk(t):
        return (t + 2 * (1 - half_x)) % 4

    def sensitivities(h, parts, t):
        q = chunk(t)
        cols = columns(q)
        first, last = parts[0] * 192, parts[-1] * 192 + 192
        field = jnp.concatenate([gt[h, i, first:last] for i in range(8)], axis=1)
        sources = jnp.dot(field, ms[:, cols], preferred_element_type=jnp.float32)
        receivers = jnp.dot(field, mr[:, cols], preferred_element_type=jnp.float32)
        gain = w_ref[:, pl.ds(pl.multiple_of(base + q * 512, 512), 512)]
        for s in parts:
            low = s * 192 - first
            dots = (
                sources[low : low + 64] * receivers[low : low + 64]
                + sources[low + 64 : low + 128] * receivers[low + 64 : low + 128]
                + sources[low + 128 : low + 192] * receivers[low + 128 : low + 192]
            )
            volumes = jnp.concatenate([vb[h, s * 64 : s * 64 + 64]] * 4, axis=1)
            a[h, s * 64 : s * 64 + 64, cols] = (gain * -(volumes * dots)).astype(jnp.bfloat16)
        if h == 0 and t < 2:
            v_copy(h, t, q, parts[0]).start()
        b_copy(h, q, parts[0]).start()
        y_copy(h, q, parts[0]).start()

    def forward(s, t):
        v_copy(0, t, chunk(t), s).wait_recv()
        c_copy(0, t, s).start()

    for t in range(4):
        sensitivities(0, [0], t)
        if t == 0:
            on_core(0, (pass_on, 1))
        if t == 1:
            on_core(1, (relay_z, 1))
    on_core(1, (wait_passed, 1))
    for t in range(4):
        sensitivities(0, [1], t)
        if t % 2:
            forward(0, t // 2)
    on_core(1, (pass_on, 0), (pass_on, 1))
    on_core(0, (wait_passed, 0), (wait_passed, 1))
    for t in range(4):
        sensitivities(1, [0, 1], t)
        if t % 2:
            forward(1, t // 2)

    def put(block, value):
        sums[0, block] = value[:, 0:128]
        sums[1, block] = value[:, 128:256]

    def a_part(half=None):
        if half is None:
            return a[...].reshape(256, 2048)
        return a[:, :, columns(half, 1024)].reshape(256, 1024)

    for t in range(2):
        v_copy(1, t, chunk(t)).start()
    whole = dot_nt(a_part(), a_part())
    put(0, whole[0:128])
    put(1, whole[128:256])

    def arrive(h):
        for s in range(2 - h):
            for q in range(4):
                b_copy(h, q, s).wait_recv()
                y_copy(h, q, s).wait_recv()
            for t in range(2):
                c_copy(h, t, s).wait_recv()

    def border(h, first):
        put(first, dot_nt(b[h], a_part()))
        put(first + 1, dot_nt(cc[h], a_part(half_x)))
        put(first + 2, dot_nt(y[h, :, columns(half_y, 1024)], a_part(half_y)))

    def core_copy(group_of):
        first, count = GROUPS[group_of]
        blocks = pl.ds(first, count)
        return send(
            sums.at[1 - c, blocks], part.at[blocks], ks.at[group_of], kr.at[group_of], partner
        )

    def add_cores(group_of):
        core_copy(group_of).wait()
        first, count = GROUPS[group_of]
        for i in range(first, first + count):
            own[i] = (sums[c, i] + part[i]).reshape(2, 4, 16, 128)

    def z_copy(i, receive=False):
        dz = (1, 3, 2)[i]
        there = (z + 4 - dz) % 4 if receive else (z + dz) % 4
        row = there if receive else z
        return send(
            own.at[pl.ds(0, 5), :, there], zparts.at[row], zs.at[i], zr.at[i],
            (ylo * 4 + there, cell),
        )

    def y_fold():
        return send(zsum.at[:, 1 - ylo], zback, zs.at[3], zr.at[3], ((1 - ylo) * 4 + z, cell))

    def fold_early():
        for i in range(3):
            z_copy(i, True).wait_recv()
        total = own[0:5, :, z]
        for i in range(3):
            total = total + zparts[(z + 4 - (1, 3, 2)[i]) % 4]
        zsum[...] = total
        y_fold().start()

    def finish_early():
        y_fold().wait()
        fin[0:5] = (zsum[:, ylo] + zback[...]) * jnp.float32(1.0 / 32768)

    def strip_copy(late, i, receive=False):
        first, count = LATER[late]
        blocks = pl.ds(first, count)
        if receive:
            there, slot = source(i), source(i)
        else:
            there, slot = peer(i), e
        return send(
            own.at[blocks, there // 4, there % 4], strips.at[slot, blocks],
            rs.at[late * 8 + i], rr.at[late * 8 + i], (there, cell),
        )

    def scatter(late):
        for i in (6, 4, 5, 3, 0, 1, 2):
            strip_copy(late, i).start()

    def gather_strips(late):
        first, count = LATER[late]
        last = first + count
        total = own[first:last, ylo, z]
        for i in range(7):
            strip_copy(late, i, True).wait_recv()
        for i in range(7):
            total = total + strips[source(i), first:last]
        fin[first:last] = total * jnp.float32(1.0 / 32768)

    def deliver(i, start):
        k, r = BLOCKS[i]
        row_half = r
        offset = pl.multiple_of(e * 16, 16)
        landing = dd.at[pl.ds(pl.multiple_of(row_half * 128 + e * 16, 16), 16)]
        row_group, col_group = group(*ROWS[k]), group(*COLS[k])
        copy = send(fin.at[i], landing, fs.at[i], fr, (row_group, col_group * 2 + c))
        if k:
            mirror = send(
                fin.at[i], tt.at[c, pl.ds(offset, 16)], ts.at[i], tr,
                (col_group, row_group * 2 + row_half),
            )
            if start:
                mirror.start()
            else:
                mirror.wait_send()
        if COLS[k] == (0, 0):
            @pl.when(row_group == e)
            def _():
                if start:
                    pltpu.make_async_copy(fin.at[i], landing, fr).start()

            @pl.when(row_group != e)
            def _():
                if start:
                    copy.start()
                else:
                    copy.wait_send()
        elif start:
            copy.start()
        else:
            copy.wait_send()

    arrive(0)
    border(0, 2)
    core_copy(0).start()
    for t in range(2):
        v_copy(1, t, chunk(t)).wait_recv()
        c_copy(1, t).start()
    add_cores(0)
    for i in range(3):
        z_copy(i).start()
    fold_early()

    def halves(ref, half):
        return ref[:, :, columns(half, 1024)].reshape(256, 1024)

    for q in range(2):
        b_copy(1, q).wait_recv()
        y_copy(1, q).wait_recv()
    border_b = dot_nt(b[1, :, 0:1024], a_part(0))
    corner_b = dot_nt(halves(y, 0), halves(b, 0))
    for q in range(2, 4):
        b_copy(1, q).wait_recv()
        y_copy(1, q).wait_recv()
    put(5, border_b + dot_nt(b[1, :, 1024:2048], a_part(1)))
    put(7, dot_nt(y[1, :, columns(half_y, 1024)], a_part(half_y)))
    for t in range(2):
        c_copy(1, t).wait_recv()
    put(6, dot_nt(cc[1], a_part(half_x)))
    core_copy(1).start()
    whole = corner_b + dot_nt(halves(y, 1), halves(b, 1))
    put(8, whole[0:128])
    put(9, whole[128:256])
    core_copy(2).start()
    whole = dot_nt(halves(y, half_x), cc[...].reshape(256, 1024))
    put(10, whole[0:128])
    put(11, whole[128:256])
    core_copy(3).start()
    for late in range(3):
        add_cores(late + 1)
        scatter(late)
    for late in range(3):
        gather_strips(late)
        if late == 0:
            finish_early()
            for i in range(5):
                deliver(i, True)
        first, count = LATER[late]
        for i in range(first, first + count):
            deliver(i, True)

    for h, s in ((0, 0), (0, 1), (1, 0)):
        for q in range(4):
            b_copy(h, q, s).wait_send()
            y_copy(h, q, s).wait_send()
        for t in range(2):
            v_copy(h, t, chunk(t), s).wait_send()
            c_copy(h, t, s).wait_send()
    for late in range(3):
        for i in range(7):
            strip_copy(late, i).wait_send()
    for s in range(2):
        for i in range(7):
            gather_copy(s, i).wait_send()
        for i in range(8):
            pass_copy(s, i, c).wait_send()
    for i in range(3):
        z_copy(i).wait_send()


    row_y, row_x = e // 4, e % 4
    dy, dx = (row_y + 2 - yhi) % 2, (row_x + 4 - x) % 4
    kind = dy * 4 + dx
    mirror_only = (kind == 3) | (kind == 5)
    straight_only = (kind == 0) | (kind == 1) | (kind == 7)

    def wait_straight():
        pltpu.make_async_copy(dd, dd, fr).wait()

    def wait_mirror():
        pltpu.make_async_copy(tt, tt, tr).wait()

    @pl.when(mirror_only)
    def _():
        wait_mirror()
        for h in range(2):
            out_ref[pl.ds(h * 128, 128)] = tt[h].T

    @pl.when(straight_only)
    def _():
        wait_straight()
        out_ref[...] = dd[...]

    @pl.when((kind == 2) | (kind == 4) | (kind == 6))
    def _():
        wait_straight()
        wait_mirror()
        for h in range(2):
            out_ref[pl.ds(h * 128, 128)] = dd[pl.ds(h * 128, 128)] + tt[h].T

    for i in range(12):
        deliver(i, False)


def per_device(grads, quads, volume, weight):
    f32, bf16 = jnp.float32, jnp.bfloat16
    dma = pltpu.SemaphoreType.DMA
    vmem = pl.BlockSpec(memory_space=pltpu.VMEM)
    return pl.pallas_call(
        kernel,
        out_shape=pltpu.VMEM((256, 128), f32),
        in_specs=[pl.BlockSpec(memory_space=pl.ANY)] * 4,
        out_specs=vmem,
        scratch_shapes=[
            pltpu.VMEM((3, 128, 128), bf16),
            pltpu.VMEM((4, 4096), jnp.int32),
            pltpu.VMEM((1, 128), f32),
            pltpu.VMEM((1, 4096), f32),
            dma((4,)),
            pltpu.VMEM((2, 8, 384, 128), bf16),
            pltpu.VMEM((2, 8, 128), f32),
            pltpu.VMEM((2, 128, 128), f32),
            pltpu.VMEM((1024, 2048), bf16),
            pltpu.VMEM((1024, 2048), bf16),
            pltpu.VMEM((2, 128, 2048), bf16),
            pltpu.VMEM((2, 128, 2048), bf16),
            pltpu.VMEM((2, 128, 1024), bf16),
            pltpu.VMEM((2, 128, 2048), bf16),
            pltpu.VMEM((2, 128, 1024), bf16),
            pltpu.VMEM((2, 12, 128, 128), f32),
            pltpu.VMEM((12, 128, 128), f32),
            pltpu.VMEM((12, 2, 4, 16, 128), f32),
            pltpu.VMEM((8, 12, 16, 128), f32),
            pltpu.VMEM((12, 16, 128), f32),
            pltpu.VMEM((256, 128), f32),
            pltpu.VMEM((2, 128, 128), f32),
            pltpu.VMEM((4, 5, 2, 16, 128), f32),
            pltpu.VMEM((5, 2, 16, 128), f32),
            pltpu.VMEM((5, 16, 128), f32),
            dma((4,)), dma((4,)), dma((14,)), dma((14,)), dma((17,)), dma((17,)),
            dma((12,)), dma((12,)), dma((12,)), dma((12,)),
            dma((6,)), dma((6,)), dma((6,)), dma((6,)),
            dma((4,)), dma((4,)), dma((24,)), dma((24,)),
            dma((12,)), dma((12,)), dma, dma,
        ],
        compiler_params=pltpu.CompilerParams(
            collective_id=0, has_side_effects=True, vmem_limit_bytes=60000000
        ),
        name="hessian",
    )(grads, quads.T, volume.reshape(1, 128), weight.reshape(1, 4096))


def solution(mesh):
    placed = (P(None, "elec", "cell"), P("elec", None), P("cell"), P("elec"))
    return jax.shard_map(
        per_device, mesh=mesh, in_specs=placed, out_specs=P("elec", "cell"), check_vma=False
    )
```
